128 devices in a mesh: row: 8 (over z_lo, y), col: 16 (over z_hi, x, core).
Axes of the slice: x: 4, y: 4, z: 4 (z_hi: 2, z_lo: 2; z = z_hi * 2 + z_lo), core: 2. Of those that a mesh axis runs over, the one named last changes fastest.
Arguments:
- slip: float32 [262144, 256], P(('row', 'col')), may hold values from -2 to 2
- state: float32 [262144, 256], P(('row', 'col')), may hold values from 0.4 to 0.9
- tau_load: float32 [262144], P(('row', 'col')), may hold values from 1 to 2
- normal_stress: float32 [262144], P(('row', 'col')), may hold values from 6 to 8
- direct_effect: float32 [262144], P(('row', 'col')), may hold values from 0.8 to 1.6
- evolution_effect: float32 [262144], P(('row', 'col')), may hold values from 0.5 to 1
- slip_distance: float32 [262144], P(('row', 'col')), may hold values from 0.5 to 2
- self_stiffness: float32 [262144], P(('row', 'col')), may hold values from 0.5 to 2
- near_blocks: bfloat16 [3, 262144, 256], P(None, ('row', 'col')), may hold values from -0.21875 to 0.21875
- basis_in: bfloat16 [32, 262144], P(None, ('row', 'col')), may hold values from -0.375 to 0.375
- basis_out: bfloat16 [32, 262144], P(None, ('row', 'col')), may hold values from -1 to 1
- coupling: bfloat16 [32768, 8, 4096], P('row', None, 'col'), may hold values from -0.046875 to 0.046875
- block_rank: int32 [1024, 8, 128], P('row', None, 'col'), may hold values from 8 to 32
- adj_bricks: int32 [8, 262144], P(None, ('row', 'col')), may hold values from 0 to 2047
- adj_count: int32 [262144], P(('row', 'col')), may hold values from 1 to 8
- adj_weight: float32 [8, 262144], P(None, ('row', 'col')), may hold values from 0.05 to 1
- pressure_now: bfloat16 [2048, 256], P('col'), may hold values from 0.099609375 to 1
- pressure_rate: bfloat16 [2048, 256], P('col'), may hold values from 0.5 to 5
Outputs:
- slip_out: float32 [262144, 256], P(('row', 'col'))
- state_out: float32 [262144, 256], P(('row', 'col'))
The draws below stay inside these ranges and needn't reach their ends.
Inputs may be any that keep to these rules, and one draw needn't show every extreme that they name: Only the first adj_count entries of a patch's brick list are read. `adj_bricks`: brick numbers index the whole reservoir. `block_rank`: ranks of pairs with |i - j| <= 1 are not read.
All inputs are finite; a program needn't handle non-finite values.
Results may differ from the reference program's by a relative error of at most 0.0007.
Values may be sent and summed in bfloat16 or wider, within the bound.
A program may use at most 192 MiB of HBM per device.

```python
import math
import jax
import jax.numpy as jnp
from jax import lax

BS = 256
R = 32
ADJ = 8
BPD = 8
ENS = 256
NBLK = 1024
PATCHES = 262144
BRICKS = 2048
N_ROW = 8
N_COL = 16


def set_ends(array, stream_key, low, top_value):
    longest = array.shape.index(max(array.shape))
    spots = []
    for shift in (0, 1):
        where = [jax.random.randint(jax.random.fold_in(stream_key, axis), (), 0, length) for axis, length in enumerate(array.shape)]
        where[longest] = (where[longest] + shift) % array.shape[longest]
        spots.append(tuple(where))
    return array.at[spots[0]].set(low).at[spots[1]].set(top_value)


def strengthened(drawn, own_key, source, target, parts, factor):
    def block_of(dim):
        return (jnp.arange(drawn.shape[dim]) // (drawn.shape[dim] // parts)).reshape((-1,) + (1,) * (drawn.ndim - 1 - dim))

    first = jax.random.permutation(own_key, parts)[block_of(target)]
    second = (block_of(target) + parts // 2) % parts
    return jnp.where((block_of(source) == first) | (block_of(source) == second), factor * drawn, drawn)


def block_levels(key, shape, pieces, low, largest):
    loudness, own = 1.0, jax.random.fold_in(key, 6)
    for dim, blocks in pieces:
        draws = jnp.exp(jax.random.uniform(jax.random.fold_in(own, dim), (blocks,), jnp.float32, low / len(pieces), largest / len(pieces)))
        loudness = loudness * jnp.repeat(draws, shape[dim] // blocks).reshape([-1 if axis == dim else 1 for axis in range(len(shape))])
    return loudness


def gaussian(own_key, extent, spread, bound, cuts=(), kind=jnp.bfloat16):
    factor_of = block_levels(own_key, extent, cuts, -0.22, 0.18) if cuts else 1.0
    values = jax.random.normal(own_key, extent, jnp.float32) * spread * factor_of
    return jnp.minimum(jnp.maximum(values, -bound), bound).astype(kind)


def noise_with(rng, shape, width, most, pieces, heavy, kind=jnp.bfloat16):
    result = width * jax.random.normal(rng, shape, jnp.float32)
    if pieces:
        result = result * block_levels(rng, shape, pieces, -0.22, 0.18)
    return jnp.clip(strengthened(result, jax.random.fold_in(rng, 3), *heavy), -most, most).astype(kind)


def setup_inputs(seed: int = 0) -> dict:
    seeds = jax.random.split(jax.random.key(seed), 19)
    return {
        "slip": gaussian(seeds[0], (PATCHES, ENS), 0.5, 2.0, ((0, 128),), jnp.float32),
        "state": jnp.clip(0.4 + 0.49999997 * jax.random.uniform(seeds[1], (PATCHES, ENS), jnp.float32) ** block_levels(seeds[1], (PATCHES, ENS), ((0, 128),), -0.2, 0.2), 0.4, 0.9),
        "tau_load": jnp.clip(1.0 + 1.0 * jax.random.uniform(seeds[2], (PATCHES,), jnp.float32) ** block_levels(seeds[2], (PATCHES,), ((0, 128),), -0.2, 0.2), 1.0, 2.0),
        "normal_stress": jnp.clip(6.0 + 2.0 * jax.random.uniform(seeds[3], (PATCHES,), jnp.float32) ** block_levels(seeds[3], (PATCHES,), ((0, 128),), -0.2, 0.2), 6.0, 8.0),
        "direct_effect": jnp.clip(jnp.exp(math.log(1.6) - 0.6931472 * jax.random.uniform(seeds[4], (PATCHES,), jnp.float32) ** block_levels(seeds[4], (PATCHES,), ((0, 128),), -0.2, 0.2)), 0.8, 1.6),
        "evolution_effect": jnp.clip(jnp.exp(math.log(1.0) - 0.6931472 * jax.random.uniform(seeds[5], (PATCHES,), jnp.float32) ** block_levels(seeds[5], (PATCHES,), ((0, 128),), -0.2, 0.2)), 0.5, 1.0),
        "slip_distance": jnp.clip(jnp.exp(math.log(2.0) - 1.3862944 * jax.random.uniform(seeds[6], (PATCHES,), jnp.float32) ** block_levels(seeds[6], (PATCHES,), ((0, 128),), -0.2, 0.2)), 0.5, 2.0),
        "self_stiffness": jnp.clip(jnp.exp(math.log(2.0) - 1.3862944 * jax.random.uniform(seeds[7], (PATCHES,), jnp.float32) ** block_levels(seeds[7], (PATCHES,), ((0, 128),), -0.2, 0.2)), 0.5, 2.0),
        "near_blocks": gaussian(seeds[8], (3, PATCHES, BS), (3 * BS) ** -0.5, 0.21875, ((1, 128),)),
        "basis_in": gaussian(seeds[9], (R, PATCHES), BS ** -0.5, 0.375, ((1, 128),)),
        "basis_out": gaussian(seeds[10], (R, PATCHES), R ** -0.5, 1.0, ((1, 128),)),
        "coupling": noise_with(seeds[11], (NBLK * R, N_ROW, N_COL * BPD * R), (NBLK * R) ** -0.5, 0.046875, ((0, 8), (2, 16)), (2, 0, 16, 2.0)),
        "block_rank": set_ends(jax.random.randint(seeds[12], (NBLK, N_ROW, N_COL * BPD), R // 4, R + 1), jax.random.fold_in(seeds[12], 1), R // 4, R).astype(jnp.int32),
        "adj_bricks": set_ends(jax.random.randint(seeds[13], (ADJ, PATCHES), 0, BRICKS), jax.random.fold_in(seeds[13], 1), 0, BRICKS - 1).astype(jnp.int32),
        "adj_count": set_ends(jax.random.randint(seeds[14], (PATCHES,), 1, ADJ + 1), jax.random.fold_in(seeds[14], 1), 1, ADJ).astype(jnp.int32),
        "adj_weight": jnp.clip(jnp.exp(math.log(1.0) - 2.9957323 * jax.random.uniform(seeds[15], (ADJ, PATCHES), jnp.float32) ** block_levels(seeds[15], (ADJ, PATCHES), ((1, 128),), -0.2, 0.2)), 0.05, 1.0),
        "pressure_now": jnp.clip(jnp.exp(math.log(1.0) - 2.306499 * jax.random.uniform(seeds[16], (BRICKS, ENS), jnp.float32) ** block_levels(seeds[16], (BRICKS, ENS), ((0, 16),), -0.2, 0.2)), 0.099609375, 1.0).astype(jnp.bfloat16),
        "pressure_rate": jnp.clip(jnp.exp(math.log(5.0) - 2.3025851 * jax.random.uniform(seeds[17], (BRICKS, ENS), jnp.float32) ** block_levels(seeds[17], (BRICKS, ENS), ((0, 16),), -0.2, 0.2)), 0.5, 5.0).astype(jnp.bfloat16),
    }


STEP_SIZE = 0.5
REF_FRICTION = 0.6


def fault_pressure(field, adj_bricks, adj_count, adj_weight):
    weight_sum = jnp.zeros(adj_count.shape, jnp.float32)
    total = jnp.zeros((adj_count.shape[0], field.shape[1]), jnp.float32)
    for slot_index in range(adj_bricks.shape[0]):
        live = (adj_count > slot_index).astype(jnp.float32)
        weighting = adj_weight[slot_index] * live
        weight_sum = weight_sum + weighting
        total = total + weighting[:, None] * field[adj_bricks[slot_index]].astype(jnp.float32)
    return total / weight_sum[:, None]


def far_mask(row_blocks, col_blocks, ranks):
    apart = jnp.abs(row_blocks[:, None] - col_blocks[None, :]) > 1
    levels = jnp.arange(R, dtype=jnp.int32)
    out_keep = levels[None, :, None, None] < ranks[:, None, :, None]
    in_keep = levels[None, None, None, :] < ranks[:, None, :, None]
    keep = apart[:, None, :, None] & out_keep & in_keep
    return keep.reshape(row_blocks.shape[0] * R, col_blocks.shape[0] * R).astype(jnp.bfloat16)


def rates(slip_now, state_now, outer, pressure, tau_load, normal_stress, direct_effect, evolution_effect, slip_distance, self_stiffness):
    tau = tau_load[:, None] - self_stiffness[:, None] * slip_now - outer
    sigma = normal_stress[:, None] - pressure
    speed = jnp.exp((tau / sigma - state_now) / direct_effect[:, None])
    drift = (evolution_effect / slip_distance)[:, None] * (jnp.exp((REF_FRICTION - state_now) / evolution_effect[:, None]) - speed)
    return speed, drift


def reference(slip, state, tau_load, normal_stress, direct_effect, evolution_effect, slip_distance, self_stiffness, near_blocks, basis_in, basis_out, coupling, block_rank, adj_bricks, adj_count, adj_weight, pressure_now, pressure_rate):
    base_press = fault_pressure(pressure_now, adj_bricks, adj_count, adj_weight)
    rate_press = fault_pressure(pressure_rate, adj_bricks, adj_count, adj_weight)
    matrix = coupling.reshape(NBLK * R, NBLK * R)
    ranks = block_rank.reshape(NBLK, NBLK)
    all_blocks = jnp.arange(NBLK, dtype=jnp.int32)
    group = 16
    near_whole = near_blocks.reshape(3, NBLK, BS, BS)

    def stress(slip_now):
        rounded = slip_now.astype(jnp.bfloat16)
        coeff = jnp.einsum("rnb,nbe->nre", basis_in.reshape(R, NBLK, BS).astype(jnp.float32), rounded.reshape(NBLK, BS, ENS).astype(jnp.float32))
        coeff = coeff.astype(jnp.bfloat16).reshape(NBLK * R, ENS)

        def row_group(group_index):
            first = group_index * group
            rows = lax.dynamic_slice_in_dim(matrix, first * R, group * R, 0)
            rank_rows = lax.dynamic_slice_in_dim(ranks, first, group, 0)
            row_blocks = first + jnp.arange(group, dtype=jnp.int32)
            masked = rows * far_mask(row_blocks, all_blocks, rank_rows)
            return jnp.dot(masked, coeff, preferred_element_type=jnp.float32)

        summed = lax.map(row_group, jnp.arange(NBLK // group, dtype=jnp.int32))
        far_coeff = summed.reshape(NBLK, R, ENS).astype(jnp.bfloat16)
        far = jnp.einsum("rnb,nre->nbe", basis_out.reshape(R, NBLK, BS).astype(jnp.float32), far_coeff.astype(jnp.float32)).reshape(PATCHES, ENS)
        blocks = rounded.reshape(NBLK, BS, ENS).astype(jnp.float32)
        zero_block = jnp.zeros((1, BS, ENS), jnp.float32)
        padded = jnp.concatenate([zero_block, blocks, zero_block], 0)
        terms = []
        for neighbour in range(3):
            terms.append(jnp.einsum("npm,nme->npe", near_whole[neighbour].astype(jnp.float32), padded[neighbour:neighbour + NBLK]))
        near = (terms[0] + terms[1] + terms[2]).reshape(PATCHES, ENS)
        return near + far

    params = (tau_load, normal_stress, direct_effect, evolution_effect, slip_distance, self_stiffness)
    speed0, drift0 = rates(slip, state, stress(slip), base_press, *params)
    slip_mid = slip + STEP_SIZE * speed0
    state_mid = state + STEP_SIZE * drift0
    speed1, drift1 = rates(slip_mid, state_mid, stress(slip_mid), base_press + STEP_SIZE * rate_press, *params)
    slip_out = slip + (0.5 * STEP_SIZE) * (speed0 + speed1)
    state_out = state + (0.5 * STEP_SIZE) * (drift0 + drift1)
    return slip_out, state_out
```

```python
import jax
import jax.numpy as jnp
from jax import lax
from jax.experimental import pallas as pl
from jax.experimental.pallas import tpu as pltpu
from jax.sharding import PartitionSpec as P

BS = 256
R = 32
BPD = 8
NPAT = 2048
ENS = 256
STEP_SIZE = 0.5
REF_FRICTION = 0.6
BF = jnp.bfloat16
F32 = jnp.float32
MESH = pl.DeviceIdType.MESH


def rows(start, size):
    return pl.ds(pl.multiple_of(start, size), size)


def kernel(
    slip_h, state_h, par_h, near_h, bin_h, bout_h, coup_h, rank_h, adj_h, adjw_h, now_h, rate_h,
    slip_o, state_o,
    cm, rm, buf, pm, rank, slip, state, nb, bin_, bout, adj, adjw, par, cols, tab, wb, press,
    s0, s1, co0, co1, part, rx0, rx1, snd, rcv0, rcv1, fc, acc_s, acc_t,
    lsem, csem, osem, a_s, a_r, h_s, h_r, p_s, p_r, p2_s, p2_r, b1_s, b1_r, b2_s, b2_r,
):
    row = lax.axis_index("row")
    col = lax.axis_index("col")
    core = lax.rem(col, 2)
    q = col // 2
    g = row * 16 + col
    partner = (row, q * 2 + 1 - core)
    after = lax.rem(g + 1, 128)
    before = lax.rem(g + 127, 128)
    after = (after // 16, lax.rem(after, 16))
    before = (before // 16, lax.rem(before, 16))
    row_peers = [(lax.rem(row + j, 8), col) for j in range(1, 8)]
    col_peers = [(row, lax.rem(q + j, 8) * 2 + core) for j in range(1, 8)]

    def remote(src, dst, send, recv, device):
        return pltpu.make_async_remote_copy(
            src_ref=src, dst_ref=dst, send_sem=send, recv_sem=recv, device_id=device, device_id_type=MESH
        )

    barrier = pltpu.get_barrier_semaphore()
    for peer in row_peers + col_peers + [partner, after, before]:
        pl.semaphore_signal(barrier, inc=1, device_id=peer, device_id_type=MESH)

    def chunk(j):
        slot = lax.rem(j, 4)
        return pltpu.make_async_copy(coup_h.at[rows(j * 1024, 1024)], buf.at[slot], csem.at[slot])

    load = {}

    def start(name, src, dst, index):
        load[name] = pltpu.make_async_copy(src, dst, lsem.at[index])
        load[name].start()

    start("slip", slip_h, slip, 0)
    start("bin", bin_h, bin_, 1)
    start("now", now_h, tab.at[q, core, :, pl.ds(0, 256)], 2)
    start("rate", rate_h, tab.at[q, core, :, pl.ds(256, 256)], 3)
    start("rank", rank_h, rank, 4)
    for j in range(3):
        chunk(j).start()
    start("par", par_h, par, 5)
    start("adj", adj_h, adj, 6)
    start("adjw", adjw_h, adjw, 7)
    start("bout", bout_h, bout, 8)

    def project(field, co, b):
        block = field[pl.ds(pl.multiple_of(b * BS + BS, BS), BS)]
        out = jnp.dot(bin_[:, rows(b * BS, BS)], block, preferred_element_type=F32)
        co[b // 4, row, rows(lax.rem(b, 4) * R, R)] = out.astype(BF)

    def gather_copies(stage, co, half):
        return [
            remote(co.at[half, row], co.at[half, row], a_s.at[stage, half, j], a_r.at[stage, half, row], row_peers[j])
            for j in range(7)
        ]

    def gather_waits(stage, co, half):
        for j in range(1, 8):
            u = lax.rem(row + 8 - j, 8)
            remote(co.at[half, u], co.at[half, u], a_s.at[stage, half, 0], a_r.at[stage, half, u], row_peers[0]).wait_recv()

    def halo_copies(stage, field):
        return [
            remote(field.at[pl.ds(BS, BS)], field.at[pl.ds(9 * BS, BS)], h_s.at[stage, 0], h_r.at[stage, 0], before),
            remote(field.at[pl.ds(8 * BS, BS)], field.at[pl.ds(0, BS)], h_s.at[stage, 1], h_r.at[stage, 1], after),
        ]

    def halo_waits(copies, field):
        for copy in copies:
            copy.wait_recv()

        @pl.when(g == 0)
        def _():
            field[pl.ds(0, BS)] = jnp.zeros((BS, ENS), BF)

        @pl.when(g == 127)
        def _():
            field[pl.ds(9 * BS, BS)] = jnp.zeros((BS, ENS), BF)

    load["slip"].wait()
    load["bin"].wait()

    @pl.loop(0, BPD)
    def _(b):
        s0[pl.ds(pl.multiple_of(b * BS + BS, BS), BS)] = slip[rows(b * BS, BS)].astype(BF)
        project(s0, co0, b)

    pl.semaphore_wait(barrier, 17)
    sends = []
    for half in range(2):
        sends += gather_copies(0, co0, half)
    halos = halo_copies(0, s0)
    sends += halos
    for copy in sends:
        copy.start()
    load["now"].wait()
    load["rate"].wait()
    own = tab.at[q, core]
    spread_p = [remote(own, own, p_s.at[j], p_r.at[q], col_peers[j]) for j in range(7)]
    for copy in spread_p:
        copy.start()

    load["rank"].wait()
    ri = lax.broadcasted_iota(jnp.int32, (256, 256), 0)
    ci = lax.broadcasted_iota(jnp.int32, (256, 256), 1)
    pm[...] = jnp.where(lax.rem(ri, 32) * 8 + ri // 32 == ci, 1.0, 0.0).astype(BF)
    spread = jnp.where(
        lax.broadcasted_iota(jnp.int32, (8, 256), 1) // 32 == lax.broadcasted_iota(jnp.int32, (8, 256), 0), 1.0, 0.0
    )
    lane = lax.broadcasted_iota(jnp.int32, (16, 8, 256), 2)
    source = lax.broadcasted_iota(jnp.int32, (16, 8, 256), 1) * 128 + col * 8 + lane // 32
    level = lax.rem(lane, 32).astype(F32)

    @pl.loop(0, 8)
    def _(t):
        wide = jnp.dot(
            rank[rows(t * 16, 16)].reshape(128, 8).astype(F32), spread, preferred_element_type=F32
        ).reshape(16, 8, 256)
        target = row * 128 + t * 16 + lax.broadcasted_iota(jnp.int32, (16, 8, 256), 0)
        limit = jnp.where((level < wide) & (jnp.abs(source - target) > 1), wide, 0.0)
        rm[rows(t * 16, 16)] = jnp.concatenate([limit, limit], 1).astype(BF)

    k_of = (
        lax.broadcasted_iota(jnp.int32, (16, 16, 256), 0) * 2 + lax.broadcasted_iota(jnp.int32, (16, 16, 256), 1) // 8
    ).astype(F32).astype(BF)

    @pl.loop(0, 32)
    def _(j):
        @pl.when(j + 3 < 32)
        def _():
            chunk(j + 3).start()

        chunk(j).wait()
        slot = lax.rem(j, 4)
        for b in range(4):
            i = j * 4 + b
            block = buf[slot, b * 256 : (b + 1) * 256].reshape(16, 16, 256)
            masked = jnp.where(k_of < rm[i][None], block, jnp.zeros((), BF)).reshape(256, 256)
            turned = jnp.dot(pm[...], masked, preferred_element_type=F32).astype(BF)
            for u in range(8):
                for half in range(2):
                    at = (half * 8 + u) * 128
                    cm[rows(i * 32, 32), at : at + 128] = turned[u * 32 : (u + 1) * 32, half * 128 : (half + 1) * 128]

    start("state", state_h, state, 9)
    for n in range(3):
        start("near" + str(n), near_h.at[n], nb.at[:, pl.ds(n * 256, 256)], 10 + n)

    def partial_sums(stage, co, rx, rcv):
        def to_partner(d):
            return remote(part.at[d, 1 - core], rx.at[d], b1_s.at[stage, d], b1_r.at[stage, d], partner)

        def to_owner(d):
            return remote(snd.at[d], rcv.at[q], b2_s.at[stage, d], b2_r.at[stage, q], (row, d * 2 + core))

        def combined(d):
            to_partner(d).wait_recv()
            return (part[d, core].astype(F32) + rx[d].astype(F32)).astype(BF)

        def flush(d):
            snd[d] = combined(d)
            to_owner(d).start()

        @pl.loop(0, 8)
        def _(s):
            d = lax.rem(q + 1 + s, 8)
            out = jnp.dot(
                cm[rows(d * 512, 512)], co[...].reshape(2048, ENS), preferred_element_type=F32
            )
            part[d] = out.reshape(2, 256, ENS).astype(BF)
            to_partner(d).start()

            @pl.when(s > 0)
            def _():
                flush(lax.rem(q + s, 8))

        rcv[q] = combined(q)

    def sums_waits(stage, rx, rcv):
        for j in range(1, 8):
            d = lax.rem(q + 8 - j, 8)
            remote(snd.at[d], rcv.at[d], b2_s.at[stage, d], b2_r.at[stage, d], partner).wait_recv()
        total = rcv[0].astype(F32)
        for d in range(1, 8):
            total = total + rcv[d].astype(F32)
        fc[...] = total.astype(BF)

    def sums_drain(stage, rx, rcv):
        for d in range(8):
            remote(part.at[d, 1 - core], rx.at[d], b1_s.at[stage, d], b1_r.at[stage, d], partner).wait_send()
        for j in range(1, 8):
            d = lax.rem(q + j, 8)
            remote(snd.at[d], rcv.at[q], b2_s.at[stage, d], b2_r.at[stage, q], partner).wait_send()

    for half in range(2):
        gather_waits(0, co0, half)
    partial_sums(0, co0, rx0, rcv0)

    for j in range(1, 8):
        d = lax.rem(q + 8 - j, 8)
        remote(tab.at[d, core], tab.at[d, core], p_s.at[0], p_r.at[d], partner).wait_recv()
    share_p = remote(tab.at[:, core], tab.at[:, core], p2_s, p2_r, partner)
    share_p.start()
    load["par"].wait()
    load["adj"].wait()
    load["adjw"].wait()
    slot_of = lax.broadcasted_iota(jnp.int32, (8, 256), 0).astype(F32)

    @pl.loop(0, BPD)
    def _(b):
        s = rows(b * BS, BS)
        p = par[:, s]
        w = jnp.where(slot_of < p[6:7], adjw[:, s], 0.0)
        w = w / jnp.sum(w, axis=0, keepdims=True)
        bricks = adj[:, s]
        hi = (bricks >> 7).astype(F32)
        lo = (bricks & 127).astype(F32)
        mixed = jnp.concatenate(
            [p[0:2], 1.0 / p[2:4], p[3:4] / p[4:5], p[5:6], p[6:8]], 0
        )
        cols[s] = jnp.concatenate([w, hi, lo, mixed], 0).T

    lanes = lax.broadcasted_iota(jnp.int32, (64, 128), 1).astype(F32).astype(BF)
    zero = jnp.zeros((), BF)

    @pl.loop(0, NPAT // 64)
    def _(t):
        s = rows(t * 64, 64)
        c = cols[s]

        def wide(k):
            return jnp.broadcast_to(c[:, k : k + 1], (64, 128)).astype(BF)

        picked = [jnp.where(wide(16 + k) == lanes, wide(k), zero) for k in range(8)]
        group = [wide(8 + k) for k in range(8)]
        for h in range(16):
            v = [jnp.where(group[k] == jnp.asarray(h, BF), picked[k], zero) for k in range(8)]
            wb[s, h * 128 : (h + 1) * 128] = ((v[0] + v[1]) + (v[2] + v[3])) + ((v[4] + v[5]) + (v[6] + v[7]))

    share_p.wait_recv()

    @pl.loop(0, 4)
    def _(t):
        s = rows(t * 512, 512)
        press[s] = jnp.dot(wb[s], tab[...].reshape(2048, 512), preferred_element_type=F32)

    load["state"].wait()
    load["bout"].wait()
    for n in range(3):
        load["near" + str(n)].wait()

    def rates(field, b, pressure, slip_now, state_now):
        s = rows(b * BS, BS)
        near = jnp.dot(nb[s], field[pl.ds(pl.multiple_of(b * BS, BS), 3 * BS)], preferred_element_type=F32)
        far = lax.dot_general(
            bout[:, s], fc[rows(b * R, R)], (((0,), (0,)), ((), ())), preferred_element_type=F32
        )
        c = cols[s]

        def column(k):
            return c[:, 24 + k : 25 + k]

        tau = column(0) - column(5) * slip_now - (near + far)
        sigma = column(1) - pressure
        speed = jnp.exp((tau / sigma - state_now) * column(2))
        drift = column(4) * (jnp.exp((REF_FRICTION - state_now) * column(3)) - speed)
        return speed, drift

    halo_waits(halos, s0)
    sums_waits(0, rx0, rcv0)
    for half in range(2):

        @pl.loop(half * 4, half * 4 + 4)
        def _(b):
            s = rows(b * BS, BS)
            slip_now, state_now = slip[s], state[s]
            speed, drift = rates(s0, b, press[s, 0:ENS], slip_now, state_now)
            acc_s[s] = slip_now + (0.5 * STEP_SIZE) * speed
            acc_t[s] = state_now + (0.5 * STEP_SIZE) * drift
            moved = slip_now + STEP_SIZE * speed
            slip[s] = moved
            state[s] = state_now + STEP_SIZE * drift
            s1[pl.ds(pl.multiple_of(b * BS + BS, BS), BS)] = moved.astype(BF)
            project(s1, co1, b)

        more = gather_copies(1, co1, half)
        for copy in more:
            copy.start()
        sends += more
    halos = halo_copies(1, s1)
    for copy in halos:
        copy.start()
    sends += halos
    sums_drain(0, rx0, rcv0)
    for half in range(2):
        gather_waits(1, co1, half)
    partial_sums(1, co1, rx1, rcv1)
    halo_waits(halos, s1)
    sums_waits(1, rx1, rcv1)

    def outs(b):
        s = rows(b * BS, BS)
        return [
            pltpu.make_async_copy(acc_s.at[s], slip_o.at[s], osem.at[0, b]),
            pltpu.make_async_copy(acc_t.at[s], state_o.at[s], osem.at[1, b]),
        ]

    @pl.loop(0, BPD)
    def _(b):
        s = rows(b * BS, BS)
        pressure = press[s, 0:ENS] + STEP_SIZE * press[s, ENS : 2 * ENS]
        speed, drift = rates(s1, b, pressure, slip[s], state[s])
        acc_s[s] = acc_s[s] + (0.5 * STEP_SIZE) * speed
        acc_t[s] = acc_t[s] + (0.5 * STEP_SIZE) * drift
        for copy in outs(b):
            copy.start()

    sums_drain(1, rx1, rcv1)
    for copy in sends + spread_p + [share_p]:
        copy.wait_send()

    @pl.loop(0, BPD)
    def _(b):
        for copy in outs(b):
            copy.wait()


def per_device(
    slip, state, tau_load, normal_stress, direct_effect, evolution_effect, slip_distance, self_stiffness,
    near_blocks, basis_in, basis_out, coupling, block_rank, adj_bricks, adj_count, adj_weight,
    pressure_now, pressure_rate,
):
    par = jnp.stack(
        [
            tau_load, normal_stress, direct_effect, evolution_effect, slip_distance, self_stiffness,
            adj_count.astype(F32), tau_load,
        ]
    )
    dma = pltpu.SemaphoreType.DMA
    vm = pltpu.VMEM
    scratch = [
        vm((4096, 2048), BF), vm((128, 16, 256), BF), vm((4, 1024, 256), BF), vm((256, 256), BF),
        vm((128, 8, 8), jnp.int32), vm((NPAT, ENS), F32), vm((NPAT, ENS), F32), vm((NPAT, 768), BF),
        vm((R, NPAT), BF), vm((R, NPAT), BF), vm((8, NPAT), jnp.int32), vm((8, NPAT), F32), vm((8, NPAT), F32),
        vm((NPAT, 32), F32), vm((8, 2, 128, 512), BF), vm((NPAT, 2048), BF), vm((NPAT, 512), F32),
        vm((2560, ENS), BF), vm((2560, ENS), BF), vm((2, 8, 128, ENS), BF), vm((2, 8, 128, ENS), BF),
        vm((8, 2, 256, ENS), BF), vm((8, 256, ENS), BF), vm((8, 256, ENS), BF), vm((8, 256, ENS), BF),
        vm((8, 256, ENS), BF), vm((8, 256, ENS), BF), vm((256, ENS), BF), vm((NPAT, ENS), F32), vm((NPAT, ENS), F32),
        dma((13,)), dma((4,)), dma((2, 8)), dma((2, 2, 7)), dma((2, 2, 8)), dma((2, 2)), dma((2, 2)),
        dma((7,)), dma((8,)), dma, dma, dma((2, 8)), dma((2, 8)), dma((2, 8)), dma((2, 8)),
    ]
    anywhere = pl.BlockSpec(memory_space=pl.ANY)
    out = jax.ShapeDtypeStruct((NPAT, ENS), F32)
    return pl.pallas_call(
        kernel,
        out_shape=(out, out),
        in_specs=[anywhere] * 12,
        out_specs=(anywhere, anywhere),
        scratch_shapes=scratch,
        compiler_params=pltpu.CompilerParams(
            collective_id=0, has_side_effects=True, vmem_limit_bytes=67043328
        ),
        name="fault_step",
    )(
        slip, state, par, near_blocks, basis_in, basis_out, coupling.reshape(-1, 256), block_rank,
        adj_bricks, adj_weight, pressure_now, pressure_rate,
    )


def solution(mesh):
    both = ("row", "col")
    vec = P(both)
    mat = P(both, None)
    lanes = P(None, both)
    in_specs = (
        mat, mat, vec, vec, vec, vec, vec, vec, P(None, both, None), lanes, lanes,
        P("row", None, "col"), P("row", None, "col"), lanes, vec, lanes, P("col", None), P("col", None),
    )
    return jax.shard_map(per_device, mesh=mesh, in_specs=in_specs, out_specs=(mat, mat), check_vma=False)
```

```python
import jax
import jax.numpy as jnp
from jax import lax
from jax.experimental import pallas as pl
from jax.experimental.pallas import tpu as pltpu
from jax.sharding import PartitionSpec as P

BS = 256
R = 32
BPD = 8
NPAT = 2048
ENS = 256
STEP_SIZE = 0.5
REF_FRICTION = 0.6
BF = jnp.bfloat16
F32 = jnp.float32
MESH = pl.DeviceIdType.MESH
VMEM = 67043328


def rows(start, size):
    return pl.ds(pl.multiple_of(start, size), size)


def kernel(
    slip_h, state_h, near_h, bin_h, bout_h, coup_h, rank_h, adj_h, adjw_h, now_h, rate_h,
    load_h, normal_h, direct_h, evolution_h, distance_h, stiffness_h, count_h,
    slip_o, state_o,
    acc_s, acc_t, cm, rm, buf, pm, pmt, rank, stress, slope, held, sigma, nb, bin_, bout, bt, adj, adjw, par, count, cols, tab, wb,
    s0, s1, co0, co1, part, rx0, rx1, snd, rcv0, rcv1, zsnd, zrcv, fc,
    lsem, csem, osem, a_s, a_r, h_s, h_r, p_s, p_r, p2_s, p2_r, b1_s, b1_r, b2_s, b2_r, z_s, z_r,
):
    row = lax.axis_index("row")
    col = lax.axis_index("col")
    core = lax.rem(col, 2)
    q = col // 2
    g = row * 16 + col
    partner = (row, q * 2 + 1 - core)
    after = lax.rem(g + 1, 128)
    before = lax.rem(g + 127, 128)
    after = (after // 16, lax.rem(after, 16))
    before = (before // 16, lax.rem(before, 16))
    zh, x = q // 4, lax.rem(q, 4)
    across = (row, lax.rem(q + 4, 8) * 2 + core)
    col_peers = [(row, (zh * 4 + lax.rem(x + j, 4)) * 2 + core) for j in range(1, 4)] + [across]

    def remote(src, dst, send, recv, device):
        return pltpu.make_async_remote_copy(
            src_ref=src, dst_ref=dst, send_sem=send, recv_sem=recv, device_id=device, device_id_type=MESH
        )

    def ring(me):
        base = (me // 4) * 4
        up, down = base + lax.rem(me + 1, 4), base + lax.rem(me + 3, 4)
        return lax.rem(me + 4, 8), up, down

    class Gather:
        def __init__(self, piece, me, device, send, recv, relay):
            self.piece, self.device, self.send, self.recv, self.relay = piece, device, send, recv, relay
            other, up, down = ring(me)
            far = (me // 4) * 4 + lax.rem(me + 2, 4)
            self.at = {"me": me, "z": other, "up": up, "down": down, "far": far}
            for name in ("up", "down", "far"):
                self.at["z" + name] = lax.rem(self.at[name] + 4, 8)
            self.open = [name for name in self.at if name != "me"]
            self.sent = []

        def copy(self, which, target, index):
            ref = self.piece(self.at[which])
            return remote(ref, ref, self.send(index), self.recv(self.at[which]), self.device(self.at[target]))

        def put(self, which, target):
            copy = self.copy(which, target, len(self.sent))
            copy.start()
            self.sent.append(copy)

        def got(self, which):
            self.copy(which, "z", 0).wait_recv()
            self.open.remove(which)

        def first(self):
            for target in ("z", "up", "down"):
                self.put("me", target)

        def second(self):
            self.got("z")
            self.put("z", "up")
            self.put("z", "down")

        def third(self):
            back, on = ("up", "down") if self.relay == "down" else ("down", "up")
            self.got(back)
            self.put(back, on)

        def fourth(self):
            back, on = ("down", "up") if self.relay == "up" else ("up", "down")
            self.got("z" + back)
            self.put("z" + back, on)

        def last(self):
            for name in list(self.open):
                self.got(name)

    row_near = [(u, col) for u in ring(row)]
    barrier = pltpu.get_barrier_semaphore()
    for peer in row_near + col_peers + [partner, after, before]:
        pl.semaphore_signal(barrier, inc=1, device_id=peer, device_id_type=MESH)

    def chunk(j):
        slot = lax.rem(j, 8)
        return pltpu.make_async_copy(coup_h.at[rows(j * 1024, 1024)], buf.at[slot], csem.at[slot])

    load = {}

    def start(name, src, dst, index):
        load[name] = pltpu.make_async_copy(src, dst, lsem.at[index])
        load[name].start()

    start("slip", slip_h, acc_s, 0)
    start("bin", bin_h, bin_, 1)
    start("now", now_h, tab.at[q, core, :, pl.ds(0, 256)], 2)
    start("rate", rate_h, tab.at[q, core, :, pl.ds(256, 256)], 3)
    start("rank", rank_h, rank, 4)
    start("adj", adj_h, adj, 5)
    start("adjw", adjw_h, adjw, 6)
    start("count", count_h, count, 7)
    params = (load_h, normal_h, direct_h, evolution_h, distance_h, stiffness_h)
    for n in range(6):
        start("par" + str(n), params[n], par.at[n], 8 + n)
    for j in range(7):
        chunk(j).start()
    start("bout", bout_h, bout, 14)

    def project(field, co, b):
        block = field[pl.ds(pl.multiple_of(b * BS + BS, BS), BS)]
        out = jnp.dot(bin_[:, rows(b * BS, BS)], block, preferred_element_type=F32)
        co[b // 4, row, rows(lax.rem(b, 4) * R, R)] = out.astype(BF)

    def coefficients(stage, co, half):
        return Gather(
            lambda u: co.at[half, u], row, lambda u: (u, col),
            lambda n: a_s.at[stage, half, n], lambda u: a_r.at[stage, half, u],
            ("up", "down")[half],
        )

    def halo_copies(stage, field):
        return [
            remote(field.at[pl.ds(BS, BS)], field.at[pl.ds(9 * BS, BS)], h_s.at[stage, 0], h_r.at[stage, 0], before),
            remote(field.at[pl.ds(8 * BS, BS)], field.at[pl.ds(0, BS)], h_s.at[stage, 1], h_r.at[stage, 1], after),
        ]

    def halo_waits(copies, field):
        for copy in copies:
            copy.wait_recv()

        @pl.when(g == 0)
        def _():
            field[pl.ds(0, BS)] = jnp.zeros((BS, ENS), BF)

        @pl.when(g == 127)
        def _():
            field[pl.ds(9 * BS, BS)] = jnp.zeros((BS, ENS), BF)

    load["slip"].wait()
    load["bin"].wait()

    @pl.loop(0, BPD)
    def _(b):
        s0[pl.ds(pl.multiple_of(b * BS + BS, BS), BS)] = acc_s[rows(b * BS, BS)].astype(BF)
        project(s0, co0, b)

    pl.semaphore_wait(barrier, 10)
    gathers0 = [coefficients(0, co0, half) for half in range(2)]
    for gather in gathers0:
        gather.first()
    halos = halo_copies(0, s0)
    sends = list(halos)
    for copy in halos:
        copy.start()
    load["now"].wait()
    load["rate"].wait()
    bricks_of = Gather(
        lambda u: tab.at[u, core], q, lambda u: (row, u * 2 + core), lambda n: p_s.at[n], lambda u: p_r.at[u],
        "both",
    )
    bricks_of.first()

    load["rank"].wait()
    ri = lax.broadcasted_iota(jnp.int32, (256, 256), 0)
    ci = lax.broadcasted_iota(jnp.int32, (256, 256), 1)
    pm[...] = jnp.where(lax.rem(ri, 32) * 8 + ri // 32 == ci, 1.0, 0.0).astype(BF)
    pmt[...] = jnp.where(lax.rem(ci, 32) * 8 + ci // 32 == ri, 1.0, 0.0).astype(BF)
    spread = jnp.where(
        lax.broadcasted_iota(jnp.int32, (8, 256), 1) // 32 == lax.broadcasted_iota(jnp.int32, (8, 256), 0), 1.0, 0.0
    )
    lane = lax.broadcasted_iota(jnp.int32, (128, 256), 1)
    apart = col * 8 + lane // 32 - row * 128 - lax.broadcasted_iota(jnp.int32, (128, 256), 0)
    level = lax.rem(lane, 32).astype(F32)
    for u in range(8):
        wide = lax.dot_general(
            rank[u].astype(F32), spread, (((0,), (0,)), ((), ())), preferred_element_type=F32
        )
        limit = jnp.where((level < wide) & (jnp.abs(apart + u * 128) > 1), wide, 0.0).astype(BF)
        for t in range(4):
            part[t, 0, u * 32 : (u + 1) * 32] = limit[t * 32 : (t + 1) * 32]
    for t in range(4):
        limit = jnp.dot(pmt[...], part[t, 0], preferred_element_type=F32).reshape(32, 8, 256)
        rm[t * 32 : (t + 1) * 32] = jnp.concatenate([limit, limit], 1).astype(BF)

    for name in ["adj", "adjw", "count"] + ["par" + str(n) for n in range(6)]:
        load[name].wait()
    slot_of = lax.broadcasted_iota(jnp.int32, (8, 128), 0)

    @pl.loop(0, 16)
    def _(t):
        s = rows(t * 128, 128)
        used = count[pl.ds(t, 1)]
        w = jnp.where(slot_of < used, adjw[:, s], 0.0)
        w = w / jnp.sum(w, axis=0, keepdims=True)
        bricks = adj[:, s]
        hi = (bricks >> 7).astype(F32)
        lo = (bricks & 127).astype(F32)
        p = [par[n, pl.ds(t, 1)] for n in range(6)]
        mixed = [p[0], p[1], 1.0 / p[2], 1.0 / p[3], p[3] / p[4], p[5], p[0], p[1]]
        cols[s] = jnp.concatenate([w, hi, lo] + mixed, 0).T

    lanes = lax.broadcasted_iota(jnp.int32, (16, 128), 1).astype(F32).astype(BF)
    zero = jnp.zeros((), BF)

    def one_hot(t):
        s = rows(t * 16, 16)
        c = cols[s]

        def wide(k):
            return jnp.broadcast_to(c[:, k : k + 1], (16, 128)).astype(BF)

        picked = [jnp.where(wide(16 + k) == lanes, wide(k), zero) for k in range(8)]
        group = [wide(8 + k) for k in range(8)]
        for h in range(16):
            v = [jnp.where(group[k] == jnp.asarray(h, BF), picked[k], zero) for k in range(8)]
            wb[s, h * 128 : (h + 1) * 128] = ((v[0] + v[1]) + (v[2] + v[3])) + ((v[4] + v[5]) + (v[6] + v[7]))

    k_of = (
        lax.broadcasted_iota(jnp.int32, (16, 16, 256), 0) * 2 + lax.broadcasted_iota(jnp.int32, (16, 16, 256), 1) // 8
    ).astype(F32).astype(BF)

    def mask_chunk(j):
        @pl.when(j + 7 < 32)
        def _():
            chunk(j + 7).start()

        chunk(j).wait()
        slot = lax.rem(j, 8)
        for b in range(4):
            i = j * 4 + b
            block = buf[slot, b * 256 : (b + 1) * 256].reshape(16, 16, 256)
            masked = jnp.where(k_of < rm[i][None], block, jnp.zeros((), BF)).reshape(256, 256)
            turned = jnp.dot(pm[...], masked, preferred_element_type=F32).astype(BF)
            one_hot(i)
            for u in range(8):
                for half in range(2):
                    at = (half * 8 + u) * 128
                    cm[rows(i * 32, 32), at : at + 128] = turned[u * 32 : (u + 1) * 32, half * 128 : (half + 1) * 128]

    def step(gathers, name):
        for gather in gathers:
            getattr(gather, name)()

    pl.loop(0, 8)(mask_chunk)
    for name in ("second", "third"):
        step(gathers0, name)
    for name in ("second", "third"):
        step([bricks_of], name)
    pl.loop(8, 16)(mask_chunk)
    step(gathers0, "fourth")
    pl.loop(16, 22)(mask_chunk)
    step([bricks_of], "fourth")
    pl.loop(22, 32)(mask_chunk)

    start("state", state_h, acc_t, 15)
    for n in range(3):
        start("near" + str(n), near_h.at[n], nb.at[:, pl.ds(n * 256, 256)], 16 + n)

    def dest(s):
        return lax.rem(zh + 1 + s // 4, 2) * 4 + lax.rem(x + 1 + lax.rem(s, 4), 4)

    def to_partner(stage, d, rx):
        return remote(part.at[d, 1 - core], rx.at[d], b1_s.at[stage, d], b1_r.at[stage, d], partner)

    def to_owner(stage, s, rcv):
        slot = (s // 4) * 4 + x
        owner = (row, (zh * 4 + lax.rem(x + 1 + lax.rem(s, 4), 4)) * 2 + core)
        return remote(snd.at[dest(s)], rcv.at[slot], b2_s.at[stage, dest(s)], b2_r.at[stage, slot], owner)

    def to_across(stage):
        return remote(zsnd.at[stage], zrcv.at[stage], z_s.at[stage], z_r.at[stage], across)

    def partial_sums(stage, co, rx, rcv):
        def combined(d):
            to_partner(stage, d, rx).wait_recv()
            return (part[d, core].astype(F32) + rx[d].astype(F32)).astype(BF)

        def flush(s):
            snd[dest(s)] = combined(dest(s))
            to_owner(stage, s, rcv).start()

        @pl.loop(0, 8)
        def _(s):
            d = dest(s)
            out = jnp.dot(
                cm[rows(d * 512, 512)], co[...].reshape(2048, ENS), preferred_element_type=F32
            )
            part[d] = out.reshape(2, 256, ENS).astype(BF)
            to_partner(stage, d, rx).start()

            @pl.when((s > 1) & (s != 5))
            def _():
                flush(s - 2)

        flush(6)
        rcv[x] = combined(dest(3))
        rcv[4 + x] = combined(dest(7))

    def arrived(stage, group, rcv):
        for j in range(1, 4):
            slot = group * 4 + lax.rem(x + j, 4)
            remote(snd.at[0], rcv.at[slot], b2_s.at[stage, 0], b2_r.at[stage, slot], partner).wait_recv()
        total = rcv[group * 4].astype(F32)
        for j in range(1, 4):
            total = total + rcv[group * 4 + j].astype(F32)
        return total

    def sums_across(stage, rcv):
        zsnd[stage] = arrived(stage, 0, rcv).astype(BF)
        to_across(stage).start()

    def sums_waits(stage, rcv):
        total = arrived(stage, 1, rcv)
        to_across(stage).wait_recv()
        fc[...] = (total + zrcv[stage].astype(F32)).astype(BF)

    def sums_drain(stage, rx, rcv):
        for d in range(8):
            to_partner(stage, d, rx).wait_send()
        for s in (0, 1, 2, 4, 5, 6):
            to_owner(stage, s, rcv).wait_send()
        to_across(stage).wait_send()

    step([bricks_of], "last")
    share_p = remote(tab.at[:, core], tab.at[:, core], p2_s, p2_r, partner)
    share_p.start()
    step(gathers0, "last")
    partial_sums(0, co0, rx0, rcv0)

    def pressures(t, which):
        s = rows(t * 512, 512)
        at = which * ENS
        field = jnp.dot(wb[s], tab[:, :, :, at : at + ENS].reshape(2048, ENS), preferred_element_type=F32)
        if which == 0:
            stiff = cols[s][:, 25:26] - field
            sigma[s] = stiff
        else:
            stiff = sigma[s] - STEP_SIZE * field
        slope[s] = cols[s][:, 26:27] / stiff

    def column(s, k):
        return cols[s][:, 24 + k : 25 + k]

    def before_far(field, b, slip_now, state_now):
        s = rows(b * BS, BS)
        near = jnp.dot(nb[s], field[pl.ds(pl.multiple_of(b * BS, BS), 3 * BS)], preferred_element_type=F32)
        stress[s] = column(s, 0) - column(s, 5) * slip_now - near
        return column(s, 4) * jnp.exp((REF_FRICTION - state_now) * column(s, 3))

    def far_part(b):
        return jnp.dot(bt[rows(b * BS, BS), 0:R], fc[rows(b * R, R)], preferred_element_type=F32)

    load["state"].wait()
    load["bout"].wait()
    for n in range(3):
        load["near" + str(n)].wait()
    share_p.wait_recv()
    pl.loop(0, 4)(lambda t: pressures(t, 0))
    sums_across(0, rcv0)
    for b in range(BPD):
        bt[b * BS : (b + 1) * BS, 0:R] = bout[:, b * BS : (b + 1) * BS].astype(F32).T.astype(BF)
    halo_waits(halos, s0)

    @pl.loop(0, BPD)
    def _(b):
        s = rows(b * BS, BS)
        held[s] = before_far(s0, b, acc_s[s], acc_t[s])

    sums_waits(0, rcv0)
    gathers1 = [coefficients(1, co1, half) for half in range(2)]
    for half in range(2):

        @pl.loop(half * 4, half * 4 + 4)
        def _(b):
            s = rows(b * BS, BS)
            slip_now, state_now = acc_s[s], acc_t[s]
            speed = jnp.exp((stress[s] - far_part(b)) * slope[s] - state_now * column(s, 2))
            drift = held[s] - column(s, 4) * speed
            moved = slip_now + STEP_SIZE * speed
            stress[s] = moved
            s1[pl.ds(pl.multiple_of(b * BS + BS, BS), BS)] = moved.astype(BF)
            held[s] = state_now + STEP_SIZE * drift
            acc_s[s] = slip_now + (0.5 * STEP_SIZE) * speed
            acc_t[s] = state_now + (0.5 * STEP_SIZE) * drift
            project(s1, co1, b)

        gathers1[half].first()

    halos = halo_copies(1, s1)
    for copy in halos:
        copy.start()
    sends += halos
    pl.loop(0, 4)(lambda t: pressures(t, 1))
    step(gathers1, "second")
    step(gathers1, "third")
    halo_waits(halos, s1)

    def before_far_1(b):
        s = rows(b * BS, BS)
        state_now = held[s]
        back = before_far(s1, b, stress[s], state_now)
        acc_t[s] = acc_t[s] + (0.5 * STEP_SIZE) * back
        held[s] = state_now * column(s, 2)

    pl.loop(0, 5)(before_far_1)
    step(gathers1, "fourth")
    pl.loop(5, BPD)(before_far_1)
    sums_drain(0, rx0, rcv0)
    step(gathers1, "last")
    partial_sums(1, co1, rx1, rcv1)
    sums_across(1, rcv1)
    sums_waits(1, rcv1)

    def outs(b):
        s = rows(b * BS, BS)
        return [
            pltpu.make_async_copy(acc_s.at[s], slip_o.at[s], osem.at[0, b]),
            pltpu.make_async_copy(acc_t.at[s], state_o.at[s], osem.at[1, b]),
        ]

    @pl.loop(0, BPD)
    def _(b):
        s = rows(b * BS, BS)
        speed = jnp.exp((stress[s] - far_part(b)) * slope[s] - held[s])
        acc_s[s] = acc_s[s] + (0.5 * STEP_SIZE) * speed
        acc_t[s] = acc_t[s] - (0.5 * STEP_SIZE) * (column(s, 4) * speed)
        for copy in outs(b):
            copy.start()

    sums_drain(1, rx1, rcv1)
    for gather in gathers0 + [bricks_of] + gathers1:
        sends += gather.sent
    for copy in sends + [share_p]:
        copy.wait_send()

    @pl.loop(0, BPD)
    def _(b):
        for copy in outs(b):
            copy.wait()


def per_device(
    slip, state, tau_load, normal_stress, direct_effect, evolution_effect, slip_distance, self_stiffness,
    near_blocks, basis_in, basis_out, coupling, block_rank, adj_bricks, adj_count, adj_weight,
    pressure_now, pressure_rate,
):
    dma = pltpu.SemaphoreType.DMA
    vm = pltpu.VMEM
    scratch = [
        vm((NPAT, ENS), F32), vm((NPAT, ENS), F32), vm((4096, 2048), BF), vm((128, 16, 256), BF), vm((8, 1024, 256), BF), vm((256, 256), BF), vm((256, 256), BF),
        vm((8, 8, 128), jnp.int32), vm((NPAT, ENS), F32), vm((NPAT, ENS), F32), vm((NPAT, ENS), F32),
        vm((NPAT, ENS), F32), vm((NPAT, 768), BF),
        vm((R, NPAT), BF), vm((R, NPAT), BF), vm((NPAT, 128), BF), vm((8, NPAT), jnp.int32), vm((8, NPAT), F32), vm((6, 16, 128), F32),
        vm((16, 128), jnp.int32), vm((NPAT, 32), F32), vm((8, 2, 128, 512), BF), vm((NPAT, 2048), BF),
        vm((2560, ENS), BF), vm((2560, ENS), BF), vm((2, 8, 128, ENS), BF), vm((2, 8, 128, ENS), BF),
        vm((8, 2, 256, ENS), BF), vm((8, 256, ENS), BF), vm((8, 256, ENS), BF), vm((8, 256, ENS), BF),
        vm((8, 256, ENS), BF), vm((8, 256, ENS), BF), vm((2, 256, ENS), BF), vm((2, 256, ENS), BF),
        vm((256, ENS), BF), dma((19,)), dma((8,)), dma((2, 8)), dma((2, 2, 7)), dma((2, 2, 8)), dma((2, 2)), dma((2, 2)),
        dma((7,)), dma((8,)), dma, dma, dma((2, 8)), dma((2, 8)), dma((2, 8)), dma((2, 8)), dma((2,)), dma((2,)),
    ]
    anywhere = pl.BlockSpec(memory_space=pl.ANY)
    out = jax.ShapeDtypeStruct((NPAT, ENS), F32)
    return pl.pallas_call(
        kernel,
        out_shape=(out, out),
        in_specs=[anywhere] * 18,
        out_specs=(anywhere, anywhere),
        scratch_shapes=scratch,
        compiler_params=pltpu.CompilerParams(
            collective_id=0, has_side_effects=True, vmem_limit_bytes=VMEM
        ),
        name="fault_step",
    )(
        slip, state, near_blocks, basis_in, basis_out, coupling.reshape(-1, 256), block_rank.transpose(1, 2, 0),
        adj_bricks, adj_weight, pressure_now, pressure_rate,
        *[
            v.reshape(16, 128)
            for v in (
                tau_load, normal_stress, direct_effect, evolution_effect, slip_distance, self_stiffness, adj_count
            )
        ],
    )


def solution(mesh):
    both = ("row", "col")
    vec = P(both)
    mat = P(both, None)
    lanes = P(None, both)
    in_specs = (
        mat, mat, vec, vec, vec, vec, vec, vec, P(None, both, None), lanes, lanes,
        P("row", None, "col"), P("row", None, "col"), lanes, vec, lanes, P("col", None), P("col", None),
    )
    return jax.shard_map(per_device, mesh=mesh, in_specs=in_specs, out_specs=(mat, mat), check_vma=False)
```

```python
import jax
import jax.numpy as jnp
from jax import lax
from jax.experimental import pallas as pl
from jax.experimental.pallas import tpu as pltpu
from jax.sharding import PartitionSpec as P

BS = 256
R = 32
BPD = 8
NPAT = 2048
ENS = 256
STEP_SIZE = 0.5
REF_FRICTION = 0.6
BF = jnp.bfloat16
F32 = jnp.float32
MESH = pl.DeviceIdType.MESH
VMEM = 67043328


def rows(start, size):
    return pl.ds(pl.multiple_of(start, size), size)


def kernel(
    slip_h, state_h, near_h, bin_h, bout_h, coup_h, rank_h, adj_h, adjw_h, now_h, rate_h,
    load_h, normal_h, direct_h, evolution_h, distance_h, stiffness_h, count_h,
    slip_o, state_o,
    acc_s, acc_t, cm, rm, buf, pm, pmt, rank, stress, slope, held, sigma, nb, bin_, bout, bt, adj, adjw, par, count, cols, tab, wb,
    s0, s1, co0, co1, part, rx0, rx1, snd, rcv0, rcv1, zsnd, zrcv, fc,
    lsem, csem, osem, a_s, a_r, h_s, h_r, p_s, p_r, p2_s, p2_r, b1_s, b1_r, b2_s, b2_r, z_s, z_r,
):
    row = lax.axis_index("row")
    col = lax.axis_index("col")
    core = lax.rem(col, 2)
    q = col // 2
    g = row * 16 + col
    partner = (row, q * 2 + 1 - core)
    after = lax.rem(g + 1, 128)
    before = lax.rem(g + 127, 128)
    after = (after // 16, lax.rem(after, 16))
    before = (before // 16, lax.rem(before, 16))
    zh, x = q // 4, lax.rem(q, 4)
    across = (row, lax.rem(q + 4, 8) * 2 + core)
    col_peers = [(row, (zh * 4 + lax.rem(x + j, 4)) * 2 + core) for j in range(1, 4)] + [across]

    def remote(src, dst, send, recv, device):
        return pltpu.make_async_remote_copy(
            src_ref=src, dst_ref=dst, send_sem=send, recv_sem=recv, device_id=device, device_id_type=MESH
        )

    def ring(me):
        base = (me // 4) * 4
        up, down = base + lax.rem(me + 1, 4), base + lax.rem(me + 3, 4)
        return lax.rem(me + 4, 8), up, down

    class Gather:
        def __init__(self, piece, me, device, send, recv, relay):
            self.piece, self.device, self.send, self.recv, self.relay = piece, device, send, recv, relay
            other, up, down = ring(me)
            far = (me // 4) * 4 + lax.rem(me + 2, 4)
            self.at = {"me": me, "z": other, "up": up, "down": down, "far": far}
            for name in ("up", "down", "far"):
                self.at["z" + name] = lax.rem(self.at[name] + 4, 8)
            self.open = [name for name in self.at if name != "me"]
            self.sent = []

        def copy(self, which, target, index):
            ref = self.piece(self.at[which])
            return remote(ref, ref, self.send(index), self.recv(self.at[which]), self.device(self.at[target]))

        def put(self, which, target):
            copy = self.copy(which, target, len(self.sent))
            copy.start()
            self.sent.append(copy)

        def got(self, which):
            self.copy(which, "z", 0).wait_recv()
            self.open.remove(which)

        def first(self):
            for target in ("z", "up", "down"):
                self.put("me", target)

        def second(self):
            self.got("z")
            self.put("z", "up")
            self.put("z", "down")

        def third(self):
            back, on = ("up", "down") if self.relay == "down" else ("down", "up")
            self.got(back)
            self.put(back, on)

        def fourth(self):
            back, on = ("down", "up") if self.relay == "up" else ("up", "down")
            self.got("z" + back)
            self.put("z" + back, on)

        def last(self):
            for name in list(self.open):
                self.got(name)

    row_near = [(u, col) for u in ring(row)]
    barrier = pltpu.get_barrier_semaphore()
    for peer in row_near + col_peers + [partner, after, before]:
        pl.semaphore_signal(barrier, inc=1, device_id=peer, device_id_type=MESH)

    def chunk(j):
        slot = lax.rem(j, 8)
        return pltpu.make_async_copy(coup_h.at[rows(j * 1024, 1024)], buf.at[slot], csem.at[slot])

    load = {}

    def start(name, src, dst, index):
        load[name] = pltpu.make_async_copy(src, dst, lsem.at[index])
        load[name].start()

    start("now", now_h, tab.at[q, core, :, pl.ds(0, 256)], 2)
    start("rate", rate_h, tab.at[q, core, :, pl.ds(256, 256)], 3)
    start("slip", slip_h, acc_s, 0)
    start("bin", bin_h, bin_, 1)
    start("rank", rank_h, rank, 4)
    start("adj", adj_h, adj, 5)
    start("adjw", adjw_h, adjw, 6)
    start("count", count_h, count, 7)
    params = (load_h, normal_h, direct_h, evolution_h, distance_h, stiffness_h)
    for n in range(6):
        start("par" + str(n), params[n], par.at[n], 8 + n)
    for j in range(7):
        chunk(j).start()
    start("bout", bout_h, bout, 14)

    def project(field, co, b):
        block = field[pl.ds(pl.multiple_of(b * BS + BS, BS), BS)]
        out = jnp.dot(bin_[:, rows(b * BS, BS)], block, preferred_element_type=F32)
        co[b // 4, row, rows(lax.rem(b, 4) * R, R)] = out.astype(BF)

    def coefficients(stage, co, half):
        return Gather(
            lambda u: co.at[half, u], row, lambda u: (u, col),
            lambda n: a_s.at[stage, half, n], lambda u: a_r.at[stage, half, u],
            ("up", "down")[half],
        )

    def halo_copies(stage, field):
        return [
            remote(field.at[pl.ds(BS, BS)], field.at[pl.ds(9 * BS, BS)], h_s.at[stage, 0], h_r.at[stage, 0], before),
            remote(field.at[pl.ds(8 * BS, BS)], field.at[pl.ds(0, BS)], h_s.at[stage, 1], h_r.at[stage, 1], after),
        ]

    def halo_waits(copies, field):
        for copy in copies:
            copy.wait_recv()

        @pl.when(g == 0)
        def _():
            field[pl.ds(0, BS)] = jnp.zeros((BS, ENS), BF)

        @pl.when(g == 127)
        def _():
            field[pl.ds(9 * BS, BS)] = jnp.zeros((BS, ENS), BF)

    load["now"].wait()
    load["rate"].wait()
    pl.semaphore_wait(barrier, 10)
    bricks_of = Gather(
        lambda u: tab.at[u, core], q, lambda u: (row, u * 2 + core), lambda n: p_s.at[n], lambda u: p_r.at[u],
        "both",
    )
    bricks_of.first()

    load["slip"].wait()
    load["bin"].wait()

    @pl.loop(0, BPD)
    def _(b):
        s0[pl.ds(pl.multiple_of(b * BS + BS, BS), BS)] = acc_s[rows(b * BS, BS)].astype(BF)
        project(s0, co0, b)

    gathers0 = [coefficients(0, co0, half) for half in range(2)]
    for gather in gathers0:
        gather.first()
    halos = halo_copies(0, s0)
    sends = list(halos)
    for copy in halos:
        copy.start()
    load["rank"].wait()
    ri = lax.broadcasted_iota(jnp.int32, (256, 256), 0)
    ci = lax.broadcasted_iota(jnp.int32, (256, 256), 1)
    pm[...] = jnp.where(lax.rem(ri, 32) * 8 + ri // 32 == ci, 1.0, 0.0).astype(BF)
    pmt[...] = jnp.where(lax.rem(ci, 32) * 8 + ci // 32 == ri, 1.0, 0.0).astype(BF)
    spread = jnp.where(
        lax.broadcasted_iota(jnp.int32, (8, 256), 1) // 32 == lax.broadcasted_iota(jnp.int32, (8, 256), 0), 1.0, 0.0
    )
    lane = lax.broadcasted_iota(jnp.int32, (128, 256), 1)
    apart = col * 8 + lane // 32 - row * 128 - lax.broadcasted_iota(jnp.int32, (128, 256), 0)
    level = lax.rem(lane, 32).astype(F32)
    for u in range(8):
        wide = lax.dot_general(
            rank[u].astype(F32), spread, (((0,), (0,)), ((), ())), preferred_element_type=F32
        )
        limit = jnp.where((level < wide) & (jnp.abs(apart + u * 128) > 1), wide, 0.0).astype(BF)
        for t in range(4):
            part[t, 0, u * 32 : (u + 1) * 32] = limit[t * 32 : (t + 1) * 32]
    for t in range(4):
        limit = jnp.dot(pmt[...], part[t, 0], preferred_element_type=F32).reshape(32, 8, 256)
        rm[t * 32 : (t + 1) * 32] = jnp.concatenate([limit, limit], 1).astype(BF)

    for name in ["adj", "adjw", "count"] + ["par" + str(n) for n in range(6)]:
        load[name].wait()
    slot_of = lax.broadcasted_iota(jnp.int32, (8, 128), 0)

    @pl.loop(0, 16)
    def _(t):
        s = rows(t * 128, 128)
        used = count[pl.ds(t, 1)]
        w = jnp.where(slot_of < used, adjw[:, s], 0.0)
        w = w / jnp.sum(w, axis=0, keepdims=True)
        bricks = adj[:, s]
        hi = (bricks >> 7).astype(F32)
        lo = (bricks & 127).astype(F32)
        p = [par[n, pl.ds(t, 1)] for n in range(6)]
        mixed = [p[0], p[1], 1.0 / p[2], 1.0 / p[3], p[3] / p[4], p[5], p[0], p[1]]
        cols[s] = jnp.concatenate([w, hi, lo] + mixed, 0).T

    lanes = lax.broadcasted_iota(jnp.int32, (16, 128), 1).astype(F32).astype(BF)
    zero = jnp.zeros((), BF)

    def one_hot(t):
        s = rows(t * 16, 16)
        c = cols[s]

        def wide(k):
            return jnp.broadcast_to(c[:, k : k + 1], (16, 128)).astype(BF)

        picked = [jnp.where(wide(16 + k) == lanes, wide(k), zero) for k in range(8)]
        group = [wide(8 + k) for k in range(8)]
        for h in range(16):
            v = [jnp.where(group[k] == jnp.asarray(h, BF), picked[k], zero) for k in range(8)]
            wb[s, h * 128 : (h + 1) * 128] = ((v[0] + v[1]) + (v[2] + v[3])) + ((v[4] + v[5]) + (v[6] + v[7]))

    k_of = (
        lax.broadcasted_iota(jnp.int32, (16, 16, 256), 0) * 2 + lax.broadcasted_iota(jnp.int32, (16, 16, 256), 1) // 8
    ).astype(F32).astype(BF)

    def mask_chunk(j):
        @pl.when(j + 7 < 32)
        def _():
            chunk(j + 7).start()

        chunk(j).wait()
        slot = lax.rem(j, 8)
        for b in range(4):
            i = j * 4 + b
            block = buf[slot, b * 256 : (b + 1) * 256].reshape(16, 16, 256)
            masked = jnp.where(k_of < rm[i][None], block, jnp.zeros((), BF)).reshape(256, 256)
            turned = jnp.dot(pm[...], masked, preferred_element_type=F32).astype(BF)
            if b < 3:
                one_hot(j * 3 + b)
            for u in range(8):
                for half in range(2):
                    at = (half * 8 + u) * 128
                    cm[rows(i * 32, 32), at : at + 128] = turned[u * 32 : (u + 1) * 32, half * 128 : (half + 1) * 128]

    def step(gathers, name):
        for gather in gathers:
            getattr(gather, name)()

    pl.loop(0, 10)(mask_chunk)
    for name in ("second", "third"):
        step([bricks_of], name)
        step(gathers0, name)
    pl.loop(10, 21)(mask_chunk)
    step([bricks_of], "fourth")
    step(gathers0, "fourth")
    pl.loop(21, 32)(mask_chunk)

    start("state", state_h, acc_t, 15)
    for n in range(3):
        start("near" + str(n), near_h.at[n], nb.at[:, pl.ds(n * 256, 256)], 16 + n)

    def dest(s):
        return lax.rem(zh + 1 + s // 4, 2) * 4 + lax.rem(x + 1 + lax.rem(s, 4), 4)

    def to_partner(stage, d, rx):
        return remote(part.at[d, 1 - core], rx.at[d], b1_s.at[stage, d], b1_r.at[stage, d], partner)

    def to_owner(stage, s, rcv):
        slot = (s // 4) * 4 + x
        owner = (row, (zh * 4 + lax.rem(x + 1 + lax.rem(s, 4), 4)) * 2 + core)
        return remote(snd.at[dest(s)], rcv.at[slot], b2_s.at[stage, dest(s)], b2_r.at[stage, slot], owner)

    def to_across(stage):
        return remote(zsnd.at[stage], zrcv.at[stage], z_s.at[stage], z_r.at[stage], across)

    def partial_sums(stage, co, rx, rcv):
        def combined(d):
            to_partner(stage, d, rx).wait_recv()
            return (part[d, core].astype(F32) + rx[d].astype(F32)).astype(BF)

        def flush(s):
            snd[dest(s)] = combined(dest(s))
            to_owner(stage, s, rcv).start()

        @pl.loop(0, 8)
        def _(s):
            d = dest(s)
            out = jnp.dot(
                cm[rows(d * 512, 512)], co[...].reshape(2048, ENS), preferred_element_type=F32
            )
            part[d] = out.reshape(2, 256, ENS).astype(BF)
            to_partner(stage, d, rx).start()

            @pl.when((s > 1) & (s != 5))
            def _():
                flush(s - 2)

        flush(6)
        rcv[x] = combined(dest(3))
        rcv[4 + x] = combined(dest(7))

    def arrived(stage, group, rcv):
        for j in range(1, 4):
            slot = group * 4 + lax.rem(x + j, 4)
            remote(snd.at[0], rcv.at[slot], b2_s.at[stage, 0], b2_r.at[stage, slot], partner).wait_recv()
        total = rcv[group * 4].astype(F32)
        for j in range(1, 4):
            total = total + rcv[group * 4 + j].astype(F32)
        return total

    def sums_across(stage, rcv):
        zsnd[stage] = arrived(stage, 0, rcv).astype(BF)
        to_across(stage).start()

    def sums_waits(stage, rcv):
        total = arrived(stage, 1, rcv)
        to_across(stage).wait_recv()
        fc[...] = (total + zrcv[stage].astype(F32)).astype(BF)

    def sums_drain(stage, rx, rcv):
        for d in range(8):
            to_partner(stage, d, rx).wait_send()
        for s in (0, 1, 2, 4, 5, 6):
            to_owner(stage, s, rcv).wait_send()
        to_across(stage).wait_send()

    step([bricks_of], "last")
    share_p = remote(tab.at[:, core], tab.at[:, core], p2_s, p2_r, partner)
    share_p.start()
    step(gathers0, "last")
    partial_sums(0, co0, rx0, rcv0)

    def one_hot_rest(t):
        for n in range(4):
            one_hot(t * 4 + n)

    pl.loop(24, 32)(one_hot_rest)
    sums_across(0, rcv0)

    def pressures(t, which):
        s = rows(t * 512, 512)
        at = which * ENS
        field = jnp.dot(wb[s], tab[:, :, :, at : at + ENS].reshape(2048, ENS), preferred_element_type=F32)
        if which == 0:
            stiff = cols[s][:, 25:26] - field
            sigma[s] = stiff
        else:
            stiff = sigma[s] - STEP_SIZE * field
        slope[s] = cols[s][:, 26:27] / stiff

    def column(s, k):
        return cols[s][:, 24 + k : 25 + k]

    def before_far(field, b, slip_now, state_now):
        s = rows(b * BS, BS)
        near = jnp.dot(nb[s], field[pl.ds(pl.multiple_of(b * BS, BS), 3 * BS)], preferred_element_type=F32)
        stress[s] = column(s, 0) - column(s, 5) * slip_now - near
        return column(s, 4) * jnp.exp((REF_FRICTION - state_now) * column(s, 3))

    def far_part(b):
        return jnp.dot(bt[rows(b * BS, BS), 0:R], fc[rows(b * R, R)], preferred_element_type=F32)

    load["state"].wait()
    load["bout"].wait()
    for n in range(3):
        load["near" + str(n)].wait()
    share_p.wait_recv()
    pl.loop(0, 4)(lambda t: pressures(t, 0))
    for b in range(BPD):
        bt[b * BS : (b + 1) * BS, 0:R] = bout[:, b * BS : (b + 1) * BS].astype(F32).T.astype(BF)
    halo_waits(halos, s0)

    @pl.loop(0, BPD)
    def _(b):
        s = rows(b * BS, BS)
        held[s] = before_far(s0, b, acc_s[s], acc_t[s])

    sums_waits(0, rcv0)
    gathers1 = [coefficients(1, co1, half) for half in range(2)]
    for half in range(2):

        @pl.loop(half * 4, half * 4 + 4)
        def _(b):
            s = rows(b * BS, BS)
            slip_now, state_now = acc_s[s], acc_t[s]
            speed = jnp.exp((stress[s] - far_part(b)) * slope[s] - state_now * column(s, 2))
            drift = held[s] - column(s, 4) * speed
            moved = slip_now + STEP_SIZE * speed
            stress[s] = moved
            s1[pl.ds(pl.multiple_of(b * BS + BS, BS), BS)] = moved.astype(BF)
            held[s] = state_now + STEP_SIZE * drift
            acc_s[s] = slip_now + (0.5 * STEP_SIZE) * speed
            acc_t[s] = state_now + (0.5 * STEP_SIZE) * drift
            project(s1, co1, b)

        gathers1[half].first()

    halos = halo_copies(1, s1)
    for copy in halos:
        copy.start()
    sends += halos
    pl.loop(0, 4)(lambda t: pressures(t, 1))
    step(gathers1, "second")
    step(gathers1, "third")
    halo_waits(halos, s1)

    def before_far_1(b):
        s = rows(b * BS, BS)
        state_now = held[s]
        back = before_far(s1, b, stress[s], state_now)
        acc_t[s] = acc_t[s] + (0.5 * STEP_SIZE) * back
        held[s] = state_now * column(s, 2)

    pl.loop(0, 5)(before_far_1)
    step(gathers1, "fourth")
    pl.loop(5, BPD)(before_far_1)
    sums_drain(0, rx0, rcv0)
    step(gathers1, "last")
    partial_sums(1, co1, rx1, rcv1)
    sums_across(1, rcv1)
    sums_waits(1, rcv1)

    def outs(b):
        s = rows(b * BS, BS)
        return [
            pltpu.make_async_copy(acc_s.at[s], slip_o.at[s], osem.at[0, b]),
            pltpu.make_async_copy(acc_t.at[s], state_o.at[s], osem.at[1, b]),
        ]

    @pl.loop(0, BPD)
    def _(b):
        s = rows(b * BS, BS)
        speed = jnp.exp((stress[s] - far_part(b)) * slope[s] - held[s])
        acc_s[s] = acc_s[s] + (0.5 * STEP_SIZE) * speed
        acc_t[s] = acc_t[s] - (0.5 * STEP_SIZE) * (column(s, 4) * speed)
        for copy in outs(b):
            copy.start()

    sums_drain(1, rx1, rcv1)
    for gather in gathers0 + [bricks_of] + gathers1:
        sends += gather.sent
    for copy in sends + [share_p]:
        copy.wait_send()

    @pl.loop(0, BPD)
    def _(b):
        for copy in outs(b):
            copy.wait()


def per_device(
    slip, state, tau_load, normal_stress, direct_effect, evolution_effect, slip_distance, self_stiffness,
    near_blocks, basis_in, basis_out, coupling, block_rank, adj_bricks, adj_count, adj_weight,
    pressure_now, pressure_rate,
):
    dma = pltpu.SemaphoreType.DMA
    vm = pltpu.VMEM
    scratch = [
        vm((NPAT, ENS), F32), vm((NPAT, ENS), F32), vm((4096, 2048), BF), vm((128, 16, 256), BF), vm((8, 1024, 256), BF), vm((256, 256), BF), vm((256, 256), BF),
        vm((8, 8, 128), jnp.int32), vm((NPAT, ENS), F32), vm((NPAT, ENS), F32), vm((NPAT, ENS), F32),
        vm((NPAT, ENS), F32), vm((NPAT, 768), BF),
        vm((R, NPAT), BF), vm((R, NPAT), BF), vm((NPAT, 128), BF), vm((8, NPAT), jnp.int32), vm((8, NPAT), F32), vm((6, 16, 128), F32),
        vm((16, 128), jnp.int32), vm((NPAT, 32), F32), vm((8, 2, 128, 512), BF), vm((NPAT, 2048), BF),
        vm((2560, ENS), BF), vm((2560, ENS), BF), vm((2, 8, 128, ENS), BF), vm((2, 8, 128, ENS), BF),
        vm((8, 2, 256, ENS), BF), vm((8, 256, ENS), BF), vm((8, 256, ENS), BF), vm((8, 256, ENS), BF),
        vm((8, 256, ENS), BF), vm((8, 256, ENS), BF), vm((2, 256, ENS), BF), vm((2, 256, ENS), BF),
        vm((256, ENS), BF), dma((19,)), dma((8,)), dma((2, 8)), dma((2, 2, 7)), dma((2, 2, 8)), dma((2, 2)), dma((2, 2)),
        dma((7,)), dma((8,)), dma, dma, dma((2, 8)), dma((2, 8)), dma((2, 8)), dma((2, 8)), dma((2,)), dma((2,)),
    ]
    anywhere = pl.BlockSpec(memory_space=pl.ANY)
    out = jax.ShapeDtypeStruct((NPAT, ENS), F32)
    return pl.pallas_call(
        kernel,
        out_shape=(out, out),
        in_specs=[anywhere] * 18,
        out_specs=(anywhere, anywhere),
        scratch_shapes=scratch,
        compiler_params=pltpu.CompilerParams(
            collective_id=0, has_side_effects=True, vmem_limit_bytes=VMEM
        ),
        name="fault_step",
    )(
        slip, state, near_blocks, basis_in, basis_out, coupling.reshape(-1, 256), block_rank.transpose(1, 2, 0),
        adj_bricks, adj_weight, pressure_now, pressure_rate,
        *[
            v.reshape(16, 128)
            for v in (
                tau_load, normal_stress, direct_effect, evolution_effect, slip_distance, self_stiffness, adj_count
            )
        ],
    )


def solution(mesh):
    both = ("row", "col")
    vec = P(both)
    mat = P(both, None)
    lanes = P(None, both)
    in_specs = (
        mat, mat, vec, vec, vec, vec, vec, vec, P(None, both, None), lanes, lanes,
        P("row", None, "col"), P("row", None, "col"), lanes, vec, lanes, P("col", None), P("col", None),
    )
    return jax.shard_map(per_device, mesh=mesh, in_specs=in_specs, out_specs=(mat, mat), check_vma=False)
```

```python
import jax
import jax.numpy as jnp
from jax import lax
from jax.experimental import pallas as pl
from jax.experimental.pallas import tpu as pltpu
from jax.sharding import PartitionSpec as P

BS = 256
R = 32
BPD = 8
NPAT = 2048
ENS = 256
STEP_SIZE = 0.5
REF_FRICTION = 0.6
BF = jnp.bfloat16
F32 = jnp.float32
MESH = pl.DeviceIdType.MESH
VMEM = 67043328


def rows(start, size):
    return pl.ds(pl.multiple_of(start, size), size)


def kernel(
    slip_h, state_h, near_h, bin_h, bout_h, coup_h, rank_h, adj_h, adjw_h, now_h, rate_h,
    load_h, normal_h, direct_h, evolution_h, distance_h, stiffness_h, count_h,
    slip_o, state_o,
    acc_s, acc_t, cm, rm, buf, pm, pmt, rank, stress, slope, held, sigma, nb, bin_, bout, bt, adj, adjw, par, count, cols, tab, wb,
    s0, s1, co0, co1, part, rx0, rx1, snd, rcv0, rcv1, zsnd, zrcv, fc,
    lsem, csem, osem, a_s, a_r, h_s, h_r, p_s, p_r, p2_s, p2_r, b1_s, b1_r, b2_s, b2_r, z_s, z_r,
):
    row = lax.axis_index("row")
    col = lax.axis_index("col")
    core = lax.rem(col, 2)
    q = col // 2
    g = row * 16 + col
    partner = (row, q * 2 + 1 - core)
    after = lax.rem(g + 1, 128)
    before = lax.rem(g + 127, 128)
    after = (after // 16, lax.rem(after, 16))
    before = (before // 16, lax.rem(before, 16))
    zh, x = q // 4, lax.rem(q, 4)
    across = (row, lax.rem(q + 4, 8) * 2 + core)
    col_peers = [(row, (zh * 4 + lax.rem(x + j, 4)) * 2 + core) for j in range(1, 4)] + [across]

    def remote(src, dst, send, recv, device):
        return pltpu.make_async_remote_copy(
            src_ref=src, dst_ref=dst, send_sem=send, recv_sem=recv, device_id=device, device_id_type=MESH
        )

    def ring(me):
        base = (me // 4) * 4
        up, down = base + lax.rem(me + 1, 4), base + lax.rem(me + 3, 4)
        return lax.rem(me + 4, 8), up, down

    class Gather:
        def __init__(self, piece, me, device, send, recv, relay):
            self.piece, self.device, self.send, self.recv, self.relay = piece, device, send, recv, relay
            other, up, down = ring(me)
            far = (me // 4) * 4 + lax.rem(me + 2, 4)
            self.at = {"me": me, "z": other, "up": up, "down": down, "far": far}
            for name in ("up", "down", "far"):
                self.at["z" + name] = lax.rem(self.at[name] + 4, 8)
            self.open = [name for name in self.at if name != "me"]
            self.sent = []

        def copy(self, which, target, index):
            ref = self.piece(self.at[which])
            return remote(ref, ref, self.send(index), self.recv(self.at[which]), self.device(self.at[target]))

        def put(self, which, target):
            copy = self.copy(which, target, len(self.sent))
            copy.start()
            self.sent.append(copy)

        def got(self, which):
            self.copy(which, "z", 0).wait_recv()
            self.open.remove(which)

        def first(self):
            for target in ("z", "up", "down"):
                self.put("me", target)

        def second(self):
            self.got("z")
            self.put("z", "up")
            self.put("z", "down")

        def third(self):
            back, on = ("up", "down") if self.relay == "down" else ("down", "up")
            self.got(back)
            self.put(back, on)

        def fourth(self):
            back, on = ("down", "up") if self.relay == "up" else ("up", "down")
            self.got("z" + back)
            self.put("z" + back, on)

        def last(self):
            for name in list(self.open):
                self.got(name)

    row_near = [(u, col) for u in ring(row)]
    barrier = pltpu.get_barrier_semaphore()
    for peer in row_near + col_peers + [partner, after, before]:
        pl.semaphore_signal(barrier, inc=1, device_id=peer, device_id_type=MESH)

    def chunk(j):
        slot = lax.rem(j, 8)
        return pltpu.make_async_copy(coup_h.at[rows(j * 1024, 1024)], buf.at[slot], csem.at[slot])

    load = {}

    def start(name, src, dst, index):
        load[name] = pltpu.make_async_copy(src, dst, lsem.at[index])
        load[name].start()

    start("now", now_h, tab.at[q, core, :, pl.ds(0, 256)], 2)
    start("rate", rate_h, tab.at[q, core, :, pl.ds(256, 256)], 3)
    start("slip", slip_h, acc_s, 0)
    start("bin", bin_h, bin_, 1)
    start("rank", rank_h, rank, 4)
    start("adj", adj_h, adj, 5)
    start("adjw", adjw_h, adjw, 6)
    start("count", count_h, count, 7)
    params = (load_h, normal_h, direct_h, evolution_h, distance_h, stiffness_h)
    for n in range(6):
        start("par" + str(n), params[n], par.at[n], 8 + n)
    for j in range(7):
        chunk(j).start()
    start("bout", bout_h, bout, 14)

    def project(field, co, b):
        block = field[pl.ds(pl.multiple_of(b * BS + BS, BS), BS)]
        out = jnp.dot(bin_[:, rows(b * BS, BS)], block, preferred_element_type=F32)
        co[b // 4, row, rows(lax.rem(b, 4) * R, R)] = out.astype(BF)

    def coefficients(stage, co, half):
        return Gather(
            lambda u: co.at[half, u], row, lambda u: (u, col),
            lambda n: a_s.at[stage, half, n], lambda u: a_r.at[stage, half, u],
            ("up", "down")[half],
        )

    def halo_copies(stage, field):
        return [
            remote(field.at[pl.ds(BS, BS)], field.at[pl.ds(9 * BS, BS)], h_s.at[stage, 0], h_r.at[stage, 0], before),
            remote(field.at[pl.ds(8 * BS, BS)], field.at[pl.ds(0, BS)], h_s.at[stage, 1], h_r.at[stage, 1], after),
        ]

    def halo_waits(copies, field):
        for copy in copies:
            copy.wait_recv()

        @pl.when(g == 0)
        def _():
            field[pl.ds(0, BS)] = jnp.zeros((BS, ENS), BF)

        @pl.when(g == 127)
        def _():
            field[pl.ds(9 * BS, BS)] = jnp.zeros((BS, ENS), BF)

    load["now"].wait()
    load["rate"].wait()
    pl.semaphore_wait(barrier, 10)
    bricks_of = Gather(
        lambda u: tab.at[u, core], q, lambda u: (row, u * 2 + core), lambda n: p_s.at[n], lambda u: p_r.at[u],
        "both",
    )
    bricks_of.first()

    load["slip"].wait()
    load["bin"].wait()

    @pl.loop(0, BPD)
    def _(b):
        s0[pl.ds(pl.multiple_of(b * BS + BS, BS), BS)] = acc_s[rows(b * BS, BS)].astype(BF)
        project(s0, co0, b)

    gathers0 = [coefficients(0, co0, half) for half in range(2)]
    for gather in gathers0:
        gather.first()
    halos = halo_copies(0, s0)
    sends = list(halos)
    for copy in halos:
        copy.start()
    load["rank"].wait()
    ri = lax.broadcasted_iota(jnp.int32, (256, 256), 0)
    ci = lax.broadcasted_iota(jnp.int32, (256, 256), 1)
    pm[...] = jnp.where(lax.rem(ri, 32) * 8 + ri // 32 == ci, 1.0, 0.0).astype(BF)
    pmt[...] = jnp.where(lax.rem(ci, 32) * 8 + ci // 32 == ri, 1.0, 0.0).astype(BF)
    spread = jnp.where(
        lax.broadcasted_iota(jnp.int32, (8, 256), 1) // 32 == lax.broadcasted_iota(jnp.int32, (8, 256), 0), 1.0, 0.0
    )
    lane = lax.broadcasted_iota(jnp.int32, (128, 256), 1)
    apart = col * 8 + lane // 32 - row * 128 - lax.broadcasted_iota(jnp.int32, (128, 256), 0)
    level = lax.rem(lane, 32).astype(F32)
    for u in range(8):
        wide = lax.dot_general(
            rank[u].astype(F32), spread, (((0,), (0,)), ((), ())), preferred_element_type=F32
        )
        limit = jnp.where((level < wide) & (jnp.abs(apart + u * 128) > 1), wide, 0.0).astype(BF)
        for t in range(4):
            part[t, 0, u * 32 : (u + 1) * 32] = limit[t * 32 : (t + 1) * 32]
    for t in range(4):
        limit = jnp.dot(pmt[...], part[t, 0], preferred_element_type=F32).reshape(32, 8, 256)
        rm[t * 32 : (t + 1) * 32] = jnp.concatenate([limit, limit], 1).astype(BF)

    for name in ["adj", "adjw", "count"] + ["par" + str(n) for n in range(6)]:
        load[name].wait()
    slot_of = lax.broadcasted_iota(jnp.int32, (8, 128), 0)

    @pl.loop(0, 16)
    def _(t):
        s = rows(t * 128, 128)
        used = count[pl.ds(t, 1)]
        w = jnp.where(slot_of < used, adjw[:, s], 0.0)
        w = w / jnp.sum(w, axis=0, keepdims=True)
        bricks = adj[:, s]
        hi = (bricks >> 7).astype(F32)
        lo = (bricks & 127).astype(F32)
        p = [par[n, pl.ds(t, 1)] for n in range(6)]
        mixed = [p[0], p[1], 1.0 / p[2], 1.0 / p[3], p[3] / p[4], p[5], p[0], p[1]]
        cols[s] = jnp.concatenate([w, hi, lo] + mixed, 0).T

    lanes = lax.broadcasted_iota(jnp.int32, (16, 128), 1).astype(F32).astype(BF)
    zero = jnp.zeros((), BF)

    def one_hot(t):
        s = rows(t * 16, 16)
        c = cols[s]

        def wide(k):
            return jnp.broadcast_to(c[:, k : k + 1], (16, 128)).astype(BF)

        picked = [jnp.where(wide(16 + k) == lanes, wide(k), zero) for k in range(8)]
        group = [wide(8 + k) for k in range(8)]
        for h in range(16):
            v = [jnp.where(group[k] == jnp.asarray(h, BF), picked[k], zero) for k in range(8)]
            wb[s, h * 128 : (h + 1) * 128] = ((v[0] + v[1]) + (v[2] + v[3])) + ((v[4] + v[5]) + (v[6] + v[7]))

    k_of = (
        lax.broadcasted_iota(jnp.int32, (16, 16, 256), 0) * 2 + lax.broadcasted_iota(jnp.int32, (16, 16, 256), 1) // 8
    ).astype(F32).astype(BF)

    def mask_chunk(j):
        @pl.when(j + 7 < 32)
        def _():
            chunk(j + 7).start()

        chunk(j).wait()
        slot = lax.rem(j, 8)
        for b in range(4):
            i = j * 4 + b
            block = buf[slot, b * 256 : (b + 1) * 256].reshape(16, 16, 256)
            masked = jnp.where(k_of < rm[i][None], block, jnp.zeros((), BF)).reshape(256, 256)
            turned = jnp.dot(pm[...], masked, preferred_element_type=F32).astype(BF)
            if b < 3:
                one_hot(j * 3 + b)
            for u in range(8):
                for half in range(2):
                    at = (half * 8 + u) * 128
                    cm[rows(i * 32, 32), at : at + 128] = turned[u * 32 : (u + 1) * 32, half * 128 : (half + 1) * 128]

    def step(gathers, name):
        for gather in gathers:
            getattr(gather, name)()

    pl.loop(0, 10)(mask_chunk)
    for name in ("second", "third"):
        step([bricks_of], name)
        step(gathers0, name)
    pl.loop(10, 21)(mask_chunk)
    step([bricks_of], "fourth")
    step(gathers0, "fourth")
    pl.loop(21, 32)(mask_chunk)

    start("state", state_h, acc_t, 15)
    for n in range(3):
        start("near" + str(n), near_h.at[n], nb.at[:, pl.ds(n * 256, 256)], 16 + n)

    def dest(s):
        return lax.rem(zh + 1 + s // 4, 2) * 4 + lax.rem(x + 1 + lax.rem(s, 4), 4)

    def to_partner(stage, d, rx):
        return remote(part.at[d, 1 - core], rx.at[d], b1_s.at[stage, d], b1_r.at[stage, d], partner)

    def to_owner(stage, s, rcv):
        slot = (s // 4) * 4 + x
        owner = (row, (zh * 4 + lax.rem(x + 1 + lax.rem(s, 4), 4)) * 2 + core)
        return remote(snd.at[dest(s)], rcv.at[slot], b2_s.at[stage, dest(s)], b2_r.at[stage, slot], owner)

    def to_across(stage):
        return remote(zsnd.at[stage], zrcv.at[stage], z_s.at[stage], z_r.at[stage], across)

    def partial_sums(stage, co, rx, rcv):
        def combined(d):
            to_partner(stage, d, rx).wait_recv()
            return (part[d, core].astype(F32) + rx[d].astype(F32)).astype(BF)

        def flush(s):
            snd[dest(s)] = combined(dest(s))
            to_owner(stage, s, rcv).start()

        @pl.loop(0, 8)
        def _(s):
            d = dest(s)
            out = jnp.dot(
                cm[rows(d * 512, 512)], co[...].reshape(2048, ENS), preferred_element_type=F32
            )
            part[d] = out.reshape(2, 256, ENS).astype(BF)
            to_partner(stage, d, rx).start()

            @pl.when((s > 1) & (s != 5))
            def _():
                flush(s - 2)

        flush(6)
        rcv[x] = combined(dest(3))
        rcv[4 + x] = combined(dest(7))

    def arrived(stage, group, rcv):
        for j in range(1, 4):
            slot = group * 4 + lax.rem(x + j, 4)
            remote(snd.at[0], rcv.at[slot], b2_s.at[stage, 0], b2_r.at[stage, slot], partner).wait_recv()
        total = rcv[group * 4].astype(F32)
        for j in range(1, 4):
            total = total + rcv[group * 4 + j].astype(F32)
        return total

    def sums_across(stage, rcv):
        zsnd[stage] = arrived(stage, 0, rcv).astype(BF)
        to_across(stage).start()

    def sums_waits(stage, rcv):
        total = arrived(stage, 1, rcv)
        to_across(stage).wait_recv()
        fc[...] = (total + zrcv[stage].astype(F32)).astype(BF)

    def sums_drain(stage, rx, rcv):
        for d in range(8):
            to_partner(stage, d, rx).wait_send()
        for s in (0, 1, 2, 4, 5, 6):
            to_owner(stage, s, rcv).wait_send()
        to_across(stage).wait_send()

    step([bricks_of], "last")
    share_p = remote(tab.at[:, core], tab.at[:, core], p2_s, p2_r, partner)
    share_p.start()
    step(gathers0, "last")
    partial_sums(0, co0, rx0, rcv0)

    def one_hot_rest(t):
        for n in range(4):
            one_hot(t * 4 + n)

    pl.loop(24, 32)(one_hot_rest)

    def pressures(t, which):
        s = rows(t * 512, 512)
        at = which * ENS
        field = jnp.dot(wb[s], tab[:, :, :, at : at + ENS].reshape(2048, ENS), preferred_element_type=F32)
        if which == 0:
            stiff = cols[s][:, 25:26] - field
            sigma[s] = stiff
        else:
            stiff = sigma[s] - STEP_SIZE * field
        slope[s] = cols[s][:, 26:27] / stiff

    def column(s, k):
        return cols[s][:, 24 + k : 25 + k]

    def before_far(field, b, slip_now, state_now):
        s = rows(b * BS, BS)
        near = jnp.dot(nb[s], field[pl.ds(pl.multiple_of(b * BS, BS), 3 * BS)], preferred_element_type=F32)
        stress[s] = column(s, 0) - column(s, 5) * slip_now - near
        return column(s, 4) * jnp.exp((REF_FRICTION - state_now) * column(s, 3))

    def far_part(b):
        return jnp.dot(bt[rows(b * BS, BS), 0:R], fc[rows(b * R, R)], preferred_element_type=F32)

    load["state"].wait()
    load["bout"].wait()
    for n in range(3):
        load["near" + str(n)].wait()
    share_p.wait_recv()
    pl.loop(0, 4)(lambda t: pressures(t, 0))
    sums_across(0, rcv0)
    for b in range(BPD):
        bt[b * BS : (b + 1) * BS, 0:R] = bout[:, b * BS : (b + 1) * BS].astype(F32).T.astype(BF)
    halo_waits(halos, s0)

    @pl.loop(0, BPD)
    def _(b):
        s = rows(b * BS, BS)
        held[s] = before_far(s0, b, acc_s[s], acc_t[s])

    sums_waits(0, rcv0)
    gathers1 = [coefficients(1, co1, half) for half in range(2)]
    for half in range(2):

        @pl.loop(half * 4, half * 4 + 4)
        def _(b):
            s = rows(b * BS, BS)
            slip_now, state_now = acc_s[s], acc_t[s]
            speed = jnp.exp((stress[s] - far_part(b)) * slope[s] - state_now * column(s, 2))
            drift = held[s] - column(s, 4) * speed
            moved = slip_now + STEP_SIZE * speed
            stress[s] = moved
            s1[pl.ds(pl.multiple_of(b * BS + BS, BS), BS)] = moved.astype(BF)
            held[s] = state_now + STEP_SIZE * drift
            acc_s[s] = slip_now + (0.5 * STEP_SIZE) * speed
            acc_t[s] = state_now + (0.5 * STEP_SIZE) * drift
            project(s1, co1, b)

        gathers1[half].first()

    halos = halo_copies(1, s1)
    for copy in halos:
        copy.start()
    sends += halos
    pl.loop(0, 4)(lambda t: pressures(t, 1))
    step(gathers1, "second")
    step(gathers1, "third")
    halo_waits(halos, s1)

    def before_far_1(b):
        s = rows(b * BS, BS)
        state_now = held[s]
        back = before_far(s1, b, stress[s], state_now)
        acc_t[s] = acc_t[s] + (0.5 * STEP_SIZE) * back
        held[s] = state_now * column(s, 2)

    pl.loop(0, 5)(before_far_1)
    step(gathers1, "fourth")
    pl.loop(5, BPD)(before_far_1)
    sums_drain(0, rx0, rcv0)
    step(gathers1, "last")
    partial_sums(1, co1, rx1, rcv1)
    sums_across(1, rcv1)
    sums_waits(1, rcv1)

    def outs(b):
        s = rows(b * BS, BS)
        return [
            pltpu.make_async_copy(acc_s.at[s], slip_o.at[s], osem.at[0, b]),
            pltpu.make_async_copy(acc_t.at[s], state_o.at[s], osem.at[1, b]),
        ]

    @pl.loop(0, BPD)
    def _(b):
        s = rows(b * BS, BS)
        speed = jnp.exp((stress[s] - far_part(b)) * slope[s] - held[s])
        acc_s[s] = acc_s[s] + (0.5 * STEP_SIZE) * speed
        acc_t[s] = acc_t[s] - (0.5 * STEP_SIZE) * (column(s, 4) * speed)
        for copy in outs(b):
            copy.start()

    sums_drain(1, rx1, rcv1)
    for gather in gathers0 + [bricks_of] + gathers1:
        sends += gather.sent
    for copy in sends + [share_p]:
        copy.wait_send()

    @pl.loop(0, BPD)
    def _(b):
        for copy in outs(b):
            copy.wait()


def per_device(
    slip, state, tau_load, normal_stress, direct_effect, evolution_effect, slip_distance, self_stiffness,
    near_blocks, basis_in, basis_out, coupling, block_rank, adj_bricks, adj_count, adj_weight,
    pressure_now, pressure_rate,
):
    dma = pltpu.SemaphoreType.DMA
    vm = pltpu.VMEM
    scratch = [
        vm((NPAT, ENS), F32), vm((NPAT, ENS), F32), vm((4096, 2048), BF), vm((128, 16, 256), BF), vm((8, 1024, 256), BF), vm((256, 256), BF), vm((256, 256), BF),
        vm((8, 8, 128), jnp.int32), vm((NPAT, ENS), F32), vm((NPAT, ENS), F32), vm((NPAT, ENS), F32),
        vm((NPAT, ENS), F32), vm((NPAT, 768), BF),
        vm((R, NPAT), BF), vm((R, NPAT), BF), vm((NPAT, 128), BF), vm((8, NPAT), jnp.int32), vm((8, NPAT), F32), vm((6, 16, 128), F32),
        vm((16, 128), jnp.int32), vm((NPAT, 32), F32), vm((8, 2, 128, 512), BF), vm((NPAT, 2048), BF),
        vm((2560, ENS), BF), vm((2560, ENS), BF), vm((2, 8, 128, ENS), BF), vm((2, 8, 128, ENS), BF),
        vm((8, 2, 256, ENS), BF), vm((8, 256, ENS), BF), vm((8, 256, ENS), BF), vm((8, 256, ENS), BF),
        vm((8, 256, ENS), BF), vm((8, 256, ENS), BF), vm((2, 256, ENS), BF), vm((2, 256, ENS), BF),
        vm((256, ENS), BF), dma((19,)), dma((8,)), dma((2, 8)), dma((2, 2, 7)), dma((2, 2, 8)), dma((2, 2)), dma((2, 2)),
        dma((7,)), dma((8,)), dma, dma, dma((2, 8)), dma((2, 8)), dma((2, 8)), dma((2, 8)), dma((2,)), dma((2,)),
    ]
    anywhere = pl.BlockSpec(memory_space=pl.ANY)
    out = jax.ShapeDtypeStruct((NPAT, ENS), F32)
    return pl.pallas_call(
        kernel,
        out_shape=(out, out),
        in_specs=[anywhere] * 18,
        out_specs=(anywhere, anywhere),
        scratch_shapes=scratch,
        compiler_params=pltpu.CompilerParams(
            collective_id=0, has_side_effects=True, vmem_limit_bytes=VMEM
        ),
        name="fault_step",
    )(
        slip, state, near_blocks, basis_in, basis_out, coupling.reshape(-1, 256), block_rank.transpose(1, 2, 0),
        adj_bricks, adj_weight, pressure_now, pressure_rate,
        *[
            v.reshape(16, 128)
            for v in (
                tau_load, normal_stress, direct_effect, evolution_effect, slip_distance, self_stiffness, adj_count
            )
        ],
    )


def solution(mesh):
    both = ("row", "col")
    vec = P(both)
    mat = P(both, None)
    lanes = P(None, both)
    in_specs = (
        mat, mat, vec, vec, vec, vec, vec, vec, P(None, both, None), lanes, lanes,
        P("row", None, "col"), P("row", None, "col"), lanes, vec, lanes, P("col", None), P("col", None),
    )
    return jax.shard_map(per_device, mesh=mesh, in_specs=in_specs, out_specs=(mat, mat), check_vma=False)
```
